32 devices in a mesh: seq: 4 (over y, x), fsdp: 8 (over z, core).
Axes of the slice: x: 2, y: 2, z: 4, core: 2. Of those that a mesh axis runs over, the one named last changes fastest.
Arguments:
- tokens: bfloat16 [8, 1152, 2048], P('fsdp', 'seq'), may hold values from -6 to 6
- doc_lengths: int32 [8, 4], P('fsdp'), may hold values from 1 to 1024, as said below
- positions: int32 [8, 1152], P('fsdp'), may hold values from 0 to 2174, as said below
- cotangent: bfloat16 [8, 1152, 2048], P('fsdp', 'seq'), may hold values from -6 to 6
- w_query: bfloat16 [2048, 2048], P('fsdp'), may hold values from -0.125 to 0.125
- key_matrix: bfloat16 [2048, 1024], P('fsdp'), may hold values from -0.125 to 0.125
- value_matrix: bfloat16 [2048, 1024], P('fsdp'), may hold values from -0.125 to 0.125
- w_attn_gate: bfloat16 [2048, 2048], P('fsdp'), may hold values from -0.125 to 0.125
- w_out: bfloat16 [2048, 2048], P('fsdp'), may hold values from -1.5 to 1.5
- w_gate: bfloat16 [2048, 6144], P('fsdp'), may hold values from -0.125 to 0.125
- w_up: bfloat16 [2048, 6144], P('fsdp'), may hold values from -0.125 to 0.125
- w_down: bfloat16 [6144, 2048], P('fsdp'), may hold values from -0.078125 to 0.078125
- gain_attn: bfloat16 [2048], P('fsdp'), may hold values from 0.25 to 1.75
- gain_mlp: bfloat16 [2048], P('fsdp'), may hold values from 0.25 to 1.75
Outputs:
- block_output: bfloat16 [8, 1152, 2048], P('fsdp', 'seq')
- grad_tokens: bfloat16 [8, 1152, 2048], P('fsdp', 'seq')
- grad_w_query: float32 [2048, 2048], P('fsdp')
- grad_w_key: float32 [2048, 1024], P('fsdp')
- grad_w_value: float32 [2048, 1024], P('fsdp')
- grad_w_attn_gate: float32 [2048, 2048], P('fsdp')
- grad_w_out: float32 [2048, 2048], P('fsdp')
- grad_w_gate: float32 [2048, 6144], P('fsdp')
- grad_w_up: float32 [2048, 6144], P('fsdp')
- grad_w_down: float32 [6144, 2048], P('fsdp')
- grad_gain_attn: float32 [2048], P('fsdp')
- grad_gain_mlp: float32 [2048], P('fsdp')
The draws below stay inside these ranges and needn't reach their ends.
Inputs may be any that keep to these rules, and one draw needn't show every extreme that they name: `doc_lengths`: each pack's 4 document lengths sum to 1152, and the largest is exactly 1024. `positions`: a token's position is its index within its document plus an offset shared by the whole document, below 1152; the longest document's offset is the largest.
All inputs are finite; a program needn't handle non-finite values.
Results may differ from the reference program's by a relative error of at most 0.02.
Values may be sent and summed in bfloat16 or wider, within the bound.
No kernel may reach another device: no remote copies, remote signals or barrier semaphores. Data moves between devices by JAX's collectives and lax.ppermute only.
A program may use at most 512 MiB of HBM per device.

```python
import jax
import jax.numpy as jnp
from jax import lax

MODEL_DIM = 2048
QUERY_HEADS = 16
KEY_VALUE_HEADS = 8
HEAD_DIM = 128
FF = 6144
NDOC = 4
PACK = 1152
PACKS = 8
LONGEST = 1024


def pack_layout(key):
    subkeys = jax.random.split(jax.random.fold_in(key, 7), 3)
    remainder = PACK - LONGEST
    cut_points = jnp.sort(jax.random.permutation(subkeys[0], remainder - 1)[:NDOC - 2] + 1).astype(jnp.int32)
    bounds = jnp.concatenate([jnp.zeros((1,), jnp.int32), cut_points, jnp.full((1,), remainder, jnp.int32)])
    pieces = bounds[1:] - bounds[:-1]
    lengths = jnp.concatenate([jnp.full((1,), LONGEST, jnp.int32), pieces])
    shuffle = jax.random.permutation(subkeys[1], NDOC)
    lengths = lengths[shuffle].astype(jnp.int32)
    offsets = jax.random.randint(subkeys[2], (NDOC,), 0, PACK).astype(jnp.int32)
    offsets = jnp.where(shuffle == 0, PACK - 1, offsets).astype(jnp.int32)
    token_index = jnp.arange(PACK, dtype=jnp.int32)
    doc_ends = jnp.cumsum(lengths).astype(jnp.int32)
    doc_index = jnp.sum((token_index[:, None] >= doc_ends[None, :]).astype(jnp.int32), axis=1)
    onehot = (doc_index[:, None] == jnp.arange(NDOC, dtype=jnp.int32)[None, :]).astype(jnp.int32)
    starts = doc_ends - lengths
    position_values = token_index - jnp.sum(onehot * starts[None, :], axis=1) + jnp.sum(onehot * offsets[None, :], axis=1)
    return (lengths, position_values.astype(jnp.int32))


def draw_doc_lengths(key, part):
    return jax.vmap(pack_layout)(jax.random.split(key, PACKS))[0]


def draw_positions(key, part):
    return jax.vmap(pack_layout)(jax.random.split(key, PACKS))[1]


def shard_levels(own_key, shape, shards, least, largest):
    def one(axis_at, blocks):
        heights = jax.random.uniform(jax.random.fold_in(jax.random.fold_in(own_key, 6), axis_at), (blocks,), jnp.float32, least / len(shards), largest / len(shards))
        return jnp.repeat(jnp.exp(heights), shape[axis_at] // blocks).reshape((-1,) + (1,) * (len(shape) - axis_at - 1))

    level = one(*shards[0])
    for cut in shards[1:]:
        level = level * one(*cut)
    return level


def bell_draw(stream_key, extent, spread, limit, cuts=(), kind=jnp.bfloat16):
    array = spread * jax.random.normal(stream_key, extent, jnp.float32)
    if cuts:
        array = array * shard_levels(stream_key, extent, cuts, -0.22, 0.18)
    return jnp.clip(array, -limit, limit).astype(kind)


def setup_inputs(seed: int = 0) -> dict:
    streams_of = jax.random.split(jax.random.key(seed), 15)
    tokens = bell_draw(streams_of[0], (PACKS, PACK, MODEL_DIM), 1.0, 6.0, ((0, 8), (1, 4)))
    doc_lengths = draw_doc_lengths(jax.random.fold_in(streams_of[14], 71), 0)
    positions = draw_positions(jax.random.fold_in(streams_of[14], 71), 0)
    cotangent = bell_draw(streams_of[3], (PACKS, PACK, MODEL_DIM), 1.0, 6.0, ((0, 8), (1, 4)))
    w_query = bell_draw(streams_of[4], (MODEL_DIM, QUERY_HEADS * HEAD_DIM), MODEL_DIM ** -0.5, 0.125, ((0, 8),))
    key_matrix = bell_draw(streams_of[5], (MODEL_DIM, KEY_VALUE_HEADS * HEAD_DIM), MODEL_DIM ** -0.5, 0.125, ((0, 8),))
    value_matrix = bell_draw(streams_of[6], (MODEL_DIM, KEY_VALUE_HEADS * HEAD_DIM), MODEL_DIM ** -0.5, 0.125, ((0, 8),))
    w_attn_gate = bell_draw(streams_of[7], (MODEL_DIM, QUERY_HEADS * HEAD_DIM), MODEL_DIM ** -0.5, 0.125, ((0, 8),))
    w_out = bell_draw(streams_of[8], (QUERY_HEADS * HEAD_DIM, MODEL_DIM), (QUERY_HEADS * HEAD_DIM // 128) ** -0.5, 1.5, ((0, 8),))
    w_gate = bell_draw(streams_of[9], (MODEL_DIM, FF), MODEL_DIM ** -0.5, 0.125, ((0, 8),))
    w_up = bell_draw(streams_of[10], (MODEL_DIM, FF), MODEL_DIM ** -0.5, 0.125, ((0, 8),))
    w_down = bell_draw(streams_of[11], (FF, MODEL_DIM), FF ** -0.5, 0.078125, ((0, 8),))
    gain_attn = jnp.clip(1.0 + 0.15 * jax.random.normal(streams_of[12], (MODEL_DIM,), jnp.float32), 0.25, 1.75).astype(jnp.bfloat16)
    gain_mlp = jnp.clip(1.0 + 0.15 * jax.random.normal(streams_of[13], (MODEL_DIM,), jnp.float32), 0.25, 1.75).astype(jnp.bfloat16)
    return {"tokens": tokens, "doc_lengths": doc_lengths, "positions": positions, "cotangent": cotangent, "w_query": w_query, "key_matrix": key_matrix, "value_matrix": value_matrix, "w_attn_gate": w_attn_gate, "w_out": w_out, "w_gate": w_gate, "w_up": w_up, "w_down": w_down, "gain_attn": gain_attn, "gain_mlp": gain_mlp}


@jax.custom_vjp
def lower_half(v):
    return lax.optimization_barrier(v.astype(jnp.bfloat16)).astype(jnp.float32)

@jax.custom_vjp
def low_back(v):
    return v

def low_keep(v):
    return (lower_half(v), None)

def low_pass(kept, grad):
    return (grad,)

def back_keep(v):
    return (v, None)

def back_low(kept, grad):
    return (lower_half(grad),)
lower_half.defvjp(low_keep, low_pass)
low_back.defvjp(back_keep, back_low)
epsilon = 1e-06
rope_base = 1000000.0
masked_value = -1e+30

def matrix_product(left_mat, right_mat):
    return jnp.dot(left_mat, right_mat, precision=lax.Precision.HIGHEST)

def sine_cosine_pair(values):
    return lower_half(low_back(values))

def rms_norm(values, gain):
    inv_scale = lax.rsqrt(lax.optimization_barrier(jnp.mean(values * values, axis=-1, keepdims=True)) + epsilon)
    return values * inv_scale * gain

def angles_of(positions):
    half_dim = HEAD_DIM // 2
    frequency = rope_base ** (-(2.0 * jnp.arange(half_dim, dtype=jnp.float32)) / HEAD_DIM)
    return positions.astype(jnp.float32)[:, None] * frequency[None, :]

def apply_rotation(values, rotary_angles):
    half_dim = values.shape[-1] // 2
    cosine = jnp.cos(rotary_angles)[:, None, :]
    sine_part = jnp.sin(rotary_angles)[:, None, :]
    leading = values[..., :half_dim]
    trailing = values[..., half_dim:]
    return jnp.concatenate([leading * cosine - trailing * sine_part, trailing * cosine + leading * sine_part], axis=-1)

def layer(params, inputs, positions, doc_lengths):
    w_query, key_matrix, value_matrix, w_attn_gate, w_out, w_gate, w_up, w_down, gain_attn, gain_mlp = params
    sequence_length = inputs.shape[0]
    token_index = jnp.arange(sequence_length, dtype=jnp.int32)
    doc_ends = jnp.cumsum(doc_lengths).astype(jnp.int32)
    segment = lax.optimization_barrier(jnp.sum((token_index[:, None] >= doc_ends[None, :]).astype(jnp.int32), axis=1))
    allowed = (segment[:, None] == segment[None, :]) & (token_index[:, None] >= token_index[None, :])
    hidden_attention = lower_half(rms_norm(inputs, gain_attn))
    query_rows = sine_cosine_pair(matrix_product(hidden_attention, w_query)).reshape(sequence_length, QUERY_HEADS, HEAD_DIM)
    every_key_row = sine_cosine_pair(matrix_product(hidden_attention, key_matrix)).reshape(sequence_length, KEY_VALUE_HEADS, HEAD_DIM)
    every_value_row = sine_cosine_pair(matrix_product(hidden_attention, value_matrix)).reshape(sequence_length, KEY_VALUE_HEADS, HEAD_DIM)
    gate_logits = sine_cosine_pair(matrix_product(hidden_attention, w_attn_gate)).reshape(sequence_length, QUERY_HEADS, HEAD_DIM)
    rotary_angles = angles_of(positions)
    rotated_query_rows = lower_half(apply_rotation(query_rows, rotary_angles)).reshape(sequence_length, KEY_VALUE_HEADS, QUERY_HEADS // KEY_VALUE_HEADS, HEAD_DIM)
    keys_rot = lower_half(apply_rotation(every_key_row, rotary_angles))
    raw_scores = low_back(jnp.einsum('qhgd,khd->hgqk', rotated_query_rows, keys_rot, precision=lax.Precision.HIGHEST))
    scores = jnp.where(allowed[None, None], raw_scores * HEAD_DIM ** (-0.5), masked_value)
    attn_probs = jax.nn.softmax(scores, axis=-1)
    mixed_heads = low_back(jnp.einsum('hgqk,khd->qhgd', lower_half(attn_probs), every_value_row, precision=lax.Precision.HIGHEST)).reshape(sequence_length, QUERY_HEADS, HEAD_DIM)
    gated_heads = sine_cosine_pair(mixed_heads * jax.nn.sigmoid(gate_logits)).reshape(sequence_length, QUERY_HEADS * HEAD_DIM)
    residual = inputs + low_back(matrix_product(gated_heads, w_out))
    h_mlp = lower_half(rms_norm(residual, gain_mlp))
    gate_pre = low_back(matrix_product(h_mlp, w_gate))
    up_pre = low_back(matrix_product(h_mlp, w_up))
    hidden = lower_half(jax.nn.silu(gate_pre) * up_pre)
    return residual + low_back(matrix_product(hidden, w_down))

def reference(tokens, doc_lengths, positions, cotangent, w_query, key_matrix, value_matrix, w_attn_gate, w_out, w_gate, w_up, w_down, gain_attn, gain_mlp):
    weights = tuple((weight_arg.astype(jnp.float32) for weight_arg in (w_query, key_matrix, value_matrix, w_attn_gate, w_out, w_gate, w_up, w_down, gain_attn, gain_mlp)))

    def one_pack(totals, packed):
        pack_tokens, pack_lengths, pack_positions, pack_cotangent = packed

        def forward(params, inputs):
            return layer(params, inputs, pack_positions, pack_lengths)
        output, pull_back = jax.vjp(forward, weights, pack_tokens.astype(jnp.float32))
        param_grads, input_grad = pull_back(pack_cotangent.astype(jnp.float32))
        totals = jax.tree.map(lambda total_grad, pack_grad: total_grad + pack_grad, totals, param_grads)
        return (totals, (output.astype(jnp.bfloat16), input_grad.astype(jnp.bfloat16)))
    zeros_init = tuple((jnp.zeros(weight_arg.shape, jnp.float32) for weight_arg in weights))
    totals, (outputs, input_grads) = lax.scan(one_pack, zeros_init, (tokens, doc_lengths, positions, cotangent))
    return (outputs, input_grads, totals[0], totals[1], totals[2], totals[3], totals[4], totals[5], totals[6], totals[7], totals[8], totals[9])
```

```python
import functools

import jax
import jax.numpy as jnp
from jax import lax
from jax.experimental import pallas as pl
from jax.experimental.pallas import tpu as pltpu
from jax.sharding import PartitionSpec as P

QUERY_HEADS = 16
KEY_VALUE_HEADS = 8
HEAD_DIM = 128
GROUP = QUERY_HEADS // KEY_VALUE_HEADS
TILE = 128

epsilon = 1e-06
rope_base = 1000000.0
masked_value = -1e30
LOG2E = 1.4426950408889634
SCALE = HEAD_DIM ** (-0.5)

f32 = jnp.float32
bf16 = jnp.bfloat16


def dot_plain(left_mat, right_mat):
    return jnp.dot(left_mat, right_mat, preferred_element_type=f32)


def dot_rows(left_mat, right_mat):
    return lax.dot_general(
        left_mat, right_mat, (((0,), (0,)), ((), ())), preferred_element_type=f32
    )


def dot_back(left_mat, right_mat):
    return lax.dot_general(
        left_mat, right_mat, (((1,), (1,)), ((), ())), preferred_element_type=f32
    )


def inv_rms(values):
    return lax.rsqrt(jnp.mean(values * values, axis=-1, keepdims=True) + epsilon)


def swap(value, bit):
    return lax.ppermute(value, "seq", [(i, i ^ bit) for i in range(4)])


def order_of(ns):
    if ns == 4:
        return lax.axis_index("seq") ^ jnp.arange(4, dtype=jnp.int32)
    return jnp.arange(ns, dtype=jnp.int32)


def gather_blocks(block, ns):
    if ns != 4:
        every = lax.all_gather(block, "seq", axis=0)
        return [every[i] for i in range(ns)]
    half = block.shape[0] // 2
    low, high = block[:half], block[half:]
    x_low = swap(low, 1)
    y_high = swap(high, 2)
    x_high = swap(high, 1)
    y_low = swap(low, 2)
    d_low = swap(x_low, 2)
    d_high = swap(y_high, 1)
    return [
        block,
        jnp.concatenate([x_low, x_high]),
        jnp.concatenate([y_low, y_high]),
        jnp.concatenate([d_low, d_high]),
    ]


def scatter_sum(partial, ns):
    if ns != 4:
        return lax.psum_scatter(partial, "seq", scatter_dimension=0, tiled=True).astype(f32)
    rows = partial.shape[0] // 4
    half = rows // 2
    own, for_x, for_y, for_d = [partial[i * rows : (i + 1) * rows] for i in range(4)]
    via_x = swap(for_d[:half], 1)
    via_y = swap(for_d[half:], 2)
    x_low = swap(for_x[:half], 1)
    y_high = swap(for_y[half:], 2)
    y_low = swap((for_y[:half].astype(f32) + via_x.astype(f32)).astype(bf16), 2)
    x_high = swap((for_x[half:].astype(f32) + via_y.astype(f32)).astype(bf16), 1)
    low = own[:half].astype(f32) + x_low.astype(f32) + y_low.astype(f32)
    high = own[half:].astype(f32) + x_high.astype(f32) + y_high.astype(f32)
    return jnp.concatenate([low, high])


def reorder(blocks):
    s = lax.axis_index("seq")
    b0, b1, b2, b3 = blocks
    odd = (s & 1) == 1
    upper = (s & 2) == 2
    c0, c1 = jnp.where(odd, b1, b0), jnp.where(odd, b0, b1)
    c2, c3 = jnp.where(odd, b3, b2), jnp.where(odd, b2, b3)
    return [
        jnp.where(upper, c2, c0),
        jnp.where(upper, c3, c1),
        jnp.where(upper, c0, c2),
        jnp.where(upper, c1, c3),
    ]


def rows_to_columns(matrix, ns):
    if ns != 4:
        return lax.all_to_all(matrix, "seq", split_axis=0, concat_axis=1, tiled=True)
    rows = matrix.shape[0] // 4
    own, for_x, for_y, for_d = reorder([matrix[i * rows : (i + 1) * rows] for i in range(4)])
    return jnp.concatenate(reorder([own, swap(for_x, 1), swap(for_y, 2), swap(for_d, 3)]), axis=1)


def columns_to_rows(matrix, ns):
    if ns != 4:
        return lax.all_to_all(matrix, "seq", split_axis=1, concat_axis=0, tiled=True)
    cols = matrix.shape[1] // 4
    own, for_x, for_y, for_d = reorder([matrix[:, i * cols : (i + 1) * cols] for i in range(4)])
    return jnp.concatenate(reorder([own, swap(for_x, 1), swap(for_y, 2), swap(for_d, 3)]), axis=0)


def turn(values, cos_part, sin_part):
    return values * cos_part + pltpu.roll(values, HEAD_DIM // 2, axis=1) * sin_part


def nt(left_mat, right_mat):
    return lax.dot_general(
        left_mat, right_mat, (((1,), (1,)), ((), ())), preferred_element_type=f32
    )


def both_heads(ref, tile):
    rows = slice(tile * TILE, (tile + 1) * TILE)
    return jnp.concatenate([ref[g, rows, :] for g in range(GROUP)], axis=0)


def masks(start_row, tile):
    shape = (TILE, GROUP * TILE)
    diag = lax.broadcasted_iota(jnp.int32, shape, 0)
    query = lax.broadcasted_iota(jnp.int32, shape, 1) % TILE
    return (diag + tile * TILE >= start_row) & (diag <= query)


def rotate_in(order, ns, rows, q_ref, k_ref, cos_ref, sin_ref, q_sc, k_sc):
    for c in range(ns):
        here = slice(c * rows, (c + 1) * rows)
        there = pl.ds(pl.multiple_of(order[c] * rows, 32), rows)
        cos_part, sin_part = cos_ref[here, :], sin_ref[here, :]
        k_sc[here, :] = turn(k_ref[there, :].astype(f32), cos_part, sin_part).astype(bf16)
        for g in range(GROUP):
            lanes = slice(g * HEAD_DIM, (g + 1) * HEAD_DIM)
            q_sc[g, here, :] = turn(q_ref[there, lanes].astype(f32), cos_part, sin_part).astype(
                bf16
            )


def forward_kernel(
    ns, order, q_ref, k_ref, v_ref, g_ref, cos_ref, sin_ref, start_ref,
    a_ref, o_ref, lse_ref, q_sc, k_sc, vt_sc, o_sc,
):
    total = q_ref.shape[0]
    rows = total // ns
    rotate_in(order, ns, rows, q_ref, k_ref, cos_ref, sin_ref, q_sc, k_sc)
    for c in range(ns):
        there = pl.ds(pl.multiple_of(order[c] * rows, 32), rows)
        o_sc[0, c * rows : (c + 1) * rows, :] = v_ref[there, :].astype(f32)
    vt_sc[...] = o_sc[0].T.astype(bf16)
    for i in range(total // TILE):
        q_tile = both_heads(q_sc, i)
        start_row = start_ref[i : i + 1, :]
        past = i * TILE
        s_diag = nt(k_sc[past : past + TILE, :], q_tile) * (SCALE * LOG2E)
        s_diag = jnp.where(masks(start_row, i), s_diag, masked_value)
        top = jnp.max(s_diag, axis=0, keepdims=True)
        if i:
            s_past = nt(k_sc[:past, :], q_tile) * (SCALE * LOG2E)
            key = lax.broadcasted_iota(jnp.int32, (past, GROUP * TILE), 0)
            s_past = jnp.where(key >= start_row, s_past, masked_value)
            top = jnp.maximum(top, jnp.max(s_past, axis=0, keepdims=True))
        p_diag = jnp.exp2(s_diag - top)
        weight = jnp.sum(p_diag, axis=0, keepdims=True)
        mixed = jnp.dot(
            vt_sc[:, past : past + TILE], p_diag.astype(bf16), preferred_element_type=f32
        )
        if i:
            p_past = jnp.exp2(s_past - top)
            weight += jnp.sum(p_past, axis=0, keepdims=True)
            mixed += jnp.dot(vt_sc[:, :past], p_past.astype(bf16), preferred_element_type=f32)
        lse_ref[0, i : i + 1, :] = top + jnp.log2(weight)
        mixed = (mixed * (1.0 / weight)).T
        for g in range(GROUP):
            o_sc[g, past : past + TILE, :] = mixed[g * TILE : (g + 1) * TILE, :]
    for c in range(ns):
        here = slice(c * rows, (c + 1) * rows)
        there = pl.ds(pl.multiple_of(order[c] * rows, 32), rows)
        for g in range(GROUP):
            lanes = slice(g * HEAD_DIM, (g + 1) * HEAD_DIM)
            o_part = o_sc[g, here, :]
            gate = jax.nn.sigmoid(g_ref[there, lanes].astype(f32))
            a_ref[there, lanes] = (o_part * gate).astype(bf16)
            o_ref[there, lanes] = o_part


def backward_kernel(
    ns, order, q_ref, k_ref, v_ref, g_ref, da_ref, o_ref, lse_ref, cos_ref, sin_ref, start_ref,
    out_ref, q_sc, k_sc, v_sc, kt_sc, do_sc, dd_sc, dq_sc, dk_sc, dv_sc,
):
    total = q_ref.shape[0]
    rows = total // ns
    step = pl.program_id(0)
    heads = pl.num_programs(0)
    wide = GROUP * HEAD_DIM
    rotate_in(order, ns, rows, q_ref, k_ref, cos_ref, sin_ref, q_sc, k_sc)

    def lanes_at(start, width):
        return pl.ds(pl.multiple_of(start, HEAD_DIM), width)

    for c in range(ns):
        here = slice(c * rows, (c + 1) * rows)
        there = pl.ds(pl.multiple_of(order[c] * rows, 32), rows)
        v_sc[here, :] = v_ref[there, :]
        for g in range(GROUP):
            lanes = slice(g * HEAD_DIM, (g + 1) * HEAD_DIM)
            gate = jax.nn.sigmoid(g_ref[there, lanes].astype(f32))
            o_part = o_ref[there, lanes]
            da_part = da_ref[there, lanes].astype(f32)
            do_part = (da_part * gate).astype(bf16)
            do_sc[g, here, :] = do_part
            dd_sc[g, here, :] = do_part.astype(f32) * o_part
            at = wide * heads + 2 * HEAD_DIM * heads + wide * step + g * HEAD_DIM
            out_ref[there, lanes_at(at, HEAD_DIM)] = (
                da_part * o_part * gate * (1.0 - gate)
            ).astype(bf16)
    kt_sc[...] = k_sc[...].astype(f32).T.astype(bf16)
    dk_sc[...] = jnp.zeros_like(dk_sc)
    dv_sc[...] = jnp.zeros_like(dv_sc)
    ones = jnp.ones((8, HEAD_DIM), f32)
    for i in range(total // TILE):
        past = i * TILE
        q_tile, do_tile = both_heads(q_sc, i), both_heads(do_sc, i)
        start_row = start_ref[i : i + 1, :]
        lse_row = lse_ref[0, i : i + 1, :]
        delta = lax.dot_general(
            ones, both_heads(dd_sc, i), (((1,), (1,)), ((), ())),
            preferred_element_type=f32, precision=lax.Precision.HIGHEST,
        )[0:1, :]
        dq_t = None
        for part in ("past", "diag") if i else ("diag",):
            keys = slice(0, past) if part == "past" else slice(past, past + TILE)
            scores = nt(k_sc[keys, :], q_tile) * (SCALE * LOG2E)
            if part == "past":
                key = lax.broadcasted_iota(jnp.int32, (past, GROUP * TILE), 0)
                allowed = key >= start_row
            else:
                allowed = masks(start_row, i)
            probs = jnp.where(allowed, jnp.exp2(scores - lse_row), 0.0)
            dprobs = nt(v_sc[keys, :], do_tile)
            dscores = (probs * (dprobs - delta)).astype(bf16)
            dv_sc[keys, :] += jnp.dot(probs.astype(bf16), do_tile, preferred_element_type=f32)
            dk_sc[keys, :] += jnp.dot(dscores, q_tile, preferred_element_type=f32)
            term = jnp.dot(kt_sc[:, keys], dscores, preferred_element_type=f32)
            dq_t = term if dq_t is None else dq_t + term
        dq_tile = dq_t.T
        for g in range(GROUP):
            dq_sc[g, past : past + TILE, :] = dq_tile[g * TILE : (g + 1) * TILE, :]
    for c in range(ns):
        here = slice(c * rows, (c + 1) * rows)
        there = pl.ds(pl.multiple_of(order[c] * rows, 32), rows)
        cos_part, sin_part = cos_ref[here, :] * SCALE, sin_ref[here, :] * (-SCALE)
        for g in range(GROUP):
            out_ref[there, lanes_at(wide * step + g * HEAD_DIM, HEAD_DIM)] = turn(
                dq_sc[g, here, :], cos_part, sin_part
            ).astype(bf16)
        out_ref[there, lanes_at(wide * heads + HEAD_DIM * step, HEAD_DIM)] = turn(
            dk_sc[here, :], cos_part, sin_part
        ).astype(bf16)
        out_ref[there, lanes_at((wide + HEAD_DIM) * heads + HEAD_DIM * step, HEAD_DIM)] = dv_sc[
            here, :
        ].astype(bf16)


def head_specs(total, heads):
    wide = GROUP * HEAD_DIM
    gate_at = (GROUP + 2) * heads // GROUP
    return [
        pl.BlockSpec((total, wide), lambda j, order: (0, j)),
        pl.BlockSpec((total, HEAD_DIM), lambda j, order: (0, GROUP * heads + j)),
        pl.BlockSpec((total, HEAD_DIM), lambda j, order: (0, (GROUP + 1) * heads + j)),
        pl.BlockSpec((total, wide), lambda j, order: (0, gate_at + j)),
    ]


def whole_block(shape):
    return pl.BlockSpec(shape, lambda *args: (0,) * len(shape))


def attend(order, packed, cos_part, sin_part, start, ns):
    total = packed.shape[0]
    heads = KEY_VALUE_HEADS // ns
    wide = GROUP * HEAD_DIM
    tiles = total // TILE
    per_head = pl.BlockSpec((total, wide), lambda j, order: (0, j))
    return pl.pallas_call(
        functools.partial(forward_kernel, ns),
        out_shape=(
            jax.ShapeDtypeStruct((total, heads * wide), bf16),
            jax.ShapeDtypeStruct((total, heads * wide), f32),
            jax.ShapeDtypeStruct((heads, tiles, GROUP * TILE), f32),
        ),
        grid_spec=pltpu.PrefetchScalarGridSpec(
            num_scalar_prefetch=1,
            grid=(heads,),
            in_specs=head_specs(total, heads)
            + [whole_block(cos_part.shape), whole_block(sin_part.shape), whole_block(start.shape)],
            out_specs=(
                per_head,
                per_head,
                pl.BlockSpec((1, tiles, GROUP * TILE), lambda j, order: (j, 0, 0)),
            ),
            scratch_shapes=[
                pltpu.VMEM((GROUP, total, HEAD_DIM), bf16),
                pltpu.VMEM((total, HEAD_DIM), bf16),
                pltpu.VMEM((HEAD_DIM, total), bf16),
                pltpu.VMEM((GROUP, total, HEAD_DIM), f32),
            ],
        ),
        cost_estimate=pl.CostEstimate(
            flops=2 * total * total * HEAD_DIM * GROUP * heads,
            bytes_accessed=10 * total * heads * wide,
            transcendentals=total * total * GROUP * heads // 2,
        ),
        name="attend",
    )(order, packed, packed, packed, packed, cos_part, sin_part, start)


def attend_back(order, packed, d_gated, mixed, lse, cos_part, sin_part, start, ns):
    total = packed.shape[0]
    heads = KEY_VALUE_HEADS // ns
    wide = GROUP * HEAD_DIM
    tiles = total // TILE
    per_head = pl.BlockSpec((total, wide), lambda j, order: (0, j))
    return pl.pallas_call(
        functools.partial(backward_kernel, ns),
        out_shape=jax.ShapeDtypeStruct(packed.shape, bf16),
        grid_spec=pltpu.PrefetchScalarGridSpec(
            num_scalar_prefetch=1,
            grid=(heads,),
            in_specs=head_specs(total, heads)
            + [
                per_head,
                per_head,
                pl.BlockSpec((1, tiles, GROUP * TILE), lambda j, order: (j, 0, 0)),
                whole_block(cos_part.shape),
                whole_block(sin_part.shape),
                whole_block(start.shape),
            ],
            out_specs=whole_block(packed.shape),
            scratch_shapes=[
                pltpu.VMEM((GROUP, total, HEAD_DIM), bf16),
                pltpu.VMEM((total, HEAD_DIM), bf16),
                pltpu.VMEM((total, HEAD_DIM), bf16),
                pltpu.VMEM((HEAD_DIM, total), bf16),
                pltpu.VMEM((GROUP, total, HEAD_DIM), bf16),
                pltpu.VMEM((GROUP, total, HEAD_DIM), f32),
                pltpu.VMEM((GROUP, total, HEAD_DIM), f32),
                pltpu.VMEM((total, HEAD_DIM), f32),
                pltpu.VMEM((total, HEAD_DIM), f32),
            ],
        ),
        cost_estimate=pl.CostEstimate(
            flops=5 * total * total * HEAD_DIM * GROUP * heads,
            bytes_accessed=16 * total * heads * wide,
            transcendentals=total * total * GROUP * heads // 2,
        ),
        name="attend_back",
    )(order, packed, packed, packed, packed, d_gated, mixed, lse, cos_part, sin_part, start)


def pick_attention_kernel(member, q_ref, k_ref, v_ref, g_ref, gain_ref, out_ref):
    at = 0
    for ref in (q_ref, k_ref, v_ref, g_ref):
        width = ref.shape[1]
        out_ref[:, at : at + width] = (ref[...].astype(f32) * gain_ref[...]).astype(bf16)
        at += width


def pick_attention(member, w_query, key_matrix, value_matrix, w_attn_gate, gain, ns):
    rows = w_query.shape[0]
    mats = (w_query, key_matrix, value_matrix, w_attn_gate)
    widths = [m.shape[1] // ns for m in mats]
    return pl.pallas_call(
        pick_attention_kernel,
        out_shape=jax.ShapeDtypeStruct((rows, sum(widths)), bf16),
        grid_spec=pltpu.PrefetchScalarGridSpec(
            num_scalar_prefetch=1,
            grid=(1,),
            in_specs=[pl.BlockSpec((rows, w), lambda i, member: (0, member[0])) for w in widths]
            + [whole_block(gain.shape)],
            out_specs=whole_block((rows, sum(widths))),
        ),
        name="pick_attention",
    )(member, *mats, gain)


def pick_units_kernel(ns, nf, member, w_ref, gain_ref, out_ref):
    unit = w_ref.shape[1] // nf
    mine = unit // ns
    for c in range(ns):

        @pl.when(member[0] == c)
        def _():
            for f in range(nf):
                at = unit * f + mine * c
                out_ref[:, mine * f : mine * (f + 1)] = (
                    w_ref[:, at : at + mine].astype(f32) * gain_ref[...]
                ).astype(bf16)


def pick_units(member, weight, gain, ns, nf):
    rows, cols = weight.shape
    step = min(rows, 64)
    return pl.pallas_call(
        functools.partial(pick_units_kernel, ns, nf),
        out_shape=jax.ShapeDtypeStruct((rows, cols // ns), bf16),
        grid_spec=pltpu.PrefetchScalarGridSpec(
            num_scalar_prefetch=1,
            grid=(rows // step,),
            in_specs=[
                pl.BlockSpec((step, cols), lambda i, member: (i, 0)),
                pl.BlockSpec((step, 1), lambda i, member: (i, 0)),
            ],
            out_specs=pl.BlockSpec((step, cols // ns), lambda i, member: (i, 0)),
        ),
        name="pick_units",
    )(member, weight, gain)


def lane_sums(values):
    out = values[:, :128]
    for at in range(128, values.shape[1], 128):
        out = out + values[:, at : at + 128]
    return out


def join_attention_kernel(ns, order, *refs):
    blocks, outs = refs[:ns], refs[ns : 2 * ns]
    q_ref, k_ref, v_ref, g_ref, gain_ref = refs[2 * ns : 2 * ns + 5]
    gq_ref, gk_ref, gv_ref, gg_ref, go_ref, gain_out, total = refs[2 * ns + 5 :]
    c = pl.program_id(0)

    @pl.when(c == 0)
    def _():
        total[...] = jnp.zeros_like(total)

    for j in range(ns):

        @pl.when(order[c] == j)
        def _():
            at = 0
            for w_ref, out_ref in (
                (q_ref, gq_ref), (k_ref, gk_ref), (v_ref, gv_ref), (g_ref, gg_ref),
            ):
                width = w_ref.shape[1]
                grad = blocks[j][:, at : at + width].astype(f32)
                out_ref[...] = grad * gain_ref[...]
                total[...] += lane_sums(grad * w_ref[...].astype(f32))
                at += width
            go_ref[...] = outs[j][...].astype(f32)

    @pl.when(c == ns - 1)
    def _():
        gain_out[...] = jnp.sum(total[...], axis=1, keepdims=True)


def join_attention(order, blocks, outs, mats, gain, ns):
    rows = gain.shape[0]
    widths = [m.shape[1] // ns for m in mats]
    out_width = outs[0].shape[1]

    def column(width):
        return pl.BlockSpec((rows, width), lambda c, order: (0, c))

    return pl.pallas_call(
        functools.partial(join_attention_kernel, ns),
        out_shape=tuple(jax.ShapeDtypeStruct(m.shape, f32) for m in mats)
        + (
            jax.ShapeDtypeStruct((rows, out_width * ns), f32),
            jax.ShapeDtypeStruct((rows, 1), f32),
        ),
        grid_spec=pltpu.PrefetchScalarGridSpec(
            num_scalar_prefetch=1,
            grid=(ns,),
            in_specs=[whole_block(b.shape) for b in blocks]
            + [whole_block(b.shape) for b in outs]
            + [column(w) for w in widths]
            + [whole_block(gain.shape)],
            out_specs=tuple(column(w) for w in widths)
            + (column(out_width), whole_block((rows, 1))),
            scratch_shapes=[pltpu.VMEM((rows, 128), f32)],
        ),
        name="join_attention",
    )(order, *blocks, *outs, *mats, gain)


def join_units_kernel(ns, nf, order, *refs):
    gates, ups = refs[:ns], refs[ns : 2 * ns]
    wg_ref, wu_ref, gain_ref = refs[2 * ns : 2 * ns + 3]
    gg_ref, gu_ref, gain_out = refs[2 * ns + 3 :]
    unit = gg_ref.shape[1] // nf
    mine = unit // ns
    total = jnp.zeros((gain_ref.shape[0], 128), f32)
    for blocks, w_ref, out_ref in ((gates, wg_ref, gg_ref), (ups, wu_ref, gu_ref)):
        for c in range(ns):
            part = blocks[0][...]
            for j in range(1, ns):
                part = jnp.where(order[c] == j, blocks[j][...], part)
            part = part.astype(f32)
            for f in range(nf):
                at = unit * f + mine * c
                out_ref[:, at : at + mine] = part[:, mine * f : mine * (f + 1)]
        grad = out_ref[...]
        total += lane_sums(grad * w_ref[...].astype(f32))
        out_ref[...] = grad * gain_ref[...]
    gain_out[...] = jnp.sum(total, axis=1, keepdims=True)


def join_units(order, gates, ups, w_gate, w_up, gain, ns, nf):
    rows, cols = w_gate.shape
    step = min(rows, 64)

    def row_block(width):
        return pl.BlockSpec((step, width), lambda i, order: (i, 0))

    return pl.pallas_call(
        functools.partial(join_units_kernel, ns, nf),
        out_shape=(
            jax.ShapeDtypeStruct((rows, cols), f32),
            jax.ShapeDtypeStruct((rows, cols), f32),
            jax.ShapeDtypeStruct((rows, 1), f32),
        ),
        grid_spec=pltpu.PrefetchScalarGridSpec(
            num_scalar_prefetch=1,
            grid=(rows // step,),
            in_specs=[row_block(cols // ns)] * (2 * ns) + [row_block(cols)] * 2 + [row_block(1)],
            out_specs=(row_block(cols), row_block(cols), row_block(1)),
        ),
        name="join_units",
    )(order, *gates, *ups, w_gate, w_up, gain)


def join_rows(order, blocks, ns):
    rows = blocks[0].shape[0]
    out = jnp.zeros((rows * ns, blocks[0].shape[1]), f32)
    for j in range(ns):
        member = order[j]
        out = lax.dynamic_update_slice(out, blocks[j].astype(f32), (member * rows, 0))
    return out


def gather_weight(shard):
    return lax.all_gather(shard, "fsdp", axis=0, tiled=True)


def scatter_grad(grad):
    return lax.psum_scatter(grad, "fsdp", scatter_dimension=0, tiled=True)


def shards(
    ns,
    nf,
    tokens,
    doc_lengths,
    positions,
    cotangent,
    w_query,
    key_matrix,
    value_matrix,
    w_attn_gate,
    w_out,
    w_gate,
    w_up,
    w_down,
    gain_attn,
    gain_mlp,
):
    member = lax.axis_index("seq").astype(jnp.int32)
    member_arr = member[None]
    order = order_of(ns)
    pack_len = positions.shape[1]
    gain_attn_f = gain_attn.astype(f32)[:, None]
    gain_mlp_f = gain_mlp.astype(f32)[:, None]
    mats = (w_query, key_matrix, value_matrix, w_attn_gate)

    w_att = gather_weight(pick_attention(member_arr, *mats, gain_attn_f, ns))
    out_cols = w_out.shape[1] // ns
    w_out_cols = gather_weight(
        lax.dynamic_slice_in_dim(w_out, member * out_cols, out_cols, axis=1)
    )
    w_out_s = rows_to_columns(w_out_cols, ns)
    w_gate_s = gather_weight(pick_units(member_arr, w_gate, gain_mlp_f, ns, nf))
    w_up_s = gather_weight(pick_units(member_arr, w_up, gain_mlp_f, ns, nf))
    down_rows = w_down.shape[0] // ns
    w_down_s = gather_weight(
        lax.dynamic_slice_in_dim(w_down, member * down_rows, down_rows, axis=0)
    )

    x_all = jnp.concatenate(gather_blocks(tokens[0], ns)).astype(f32)
    n_all = (x_all * inv_rms(x_all)).astype(bf16)
    e_all = jnp.concatenate(gather_blocks(cotangent[0], ns))

    token_index = jnp.arange(pack_len, dtype=jnp.int32)
    doc_ends = jnp.cumsum(doc_lengths[0])
    start = jnp.max(
        jnp.where(token_index[:, None] >= doc_ends[None, :], doc_ends[None, :], 0), axis=1
    ).astype(jnp.int32)
    start = jnp.tile(start.reshape(pack_len // TILE, TILE), (1, GROUP))
    frequency = rope_base ** (-(2.0 * jnp.arange(HEAD_DIM // 2, dtype=f32)) / HEAD_DIM)
    angles = positions[0].astype(f32)[:, None] * frequency[None, :]
    cos_part = jnp.concatenate([jnp.cos(angles)] * 2, axis=1)
    sine = jnp.sin(angles)
    sin_part = jnp.concatenate([-sine, sine], axis=1)

    packed = dot_plain(n_all, w_att).astype(bf16)
    gated, mixed, lse = attend(order, packed, cos_part, sin_part, start, ns)
    inputs = tokens[0].astype(f32)
    residual = inputs + scatter_sum(dot_plain(gated, w_out_s).astype(bf16), ns)

    scale_mlp = inv_rms(residual)
    normed_mlp = residual * scale_mlp
    m_all = jnp.concatenate(gather_blocks(normed_mlp.astype(bf16), ns))
    gate_pre = dot_plain(m_all, w_gate_s)
    up_pre = dot_plain(m_all, w_up_s)
    sig_gate = jax.nn.sigmoid(gate_pre)
    silu_gate = gate_pre * sig_gate
    hidden = (silu_gate * up_pre).astype(bf16)
    grad_hidden = dot_back(e_all, w_down_s)
    d_gate = (grad_hidden * up_pre * sig_gate * (1.0 + gate_pre * (1.0 - sig_gate))).astype(bf16)
    d_up = (grad_hidden * silu_gate).astype(bf16)
    g_down = scatter_grad(dot_rows(hidden, e_all).astype(bf16))
    d_normed = scatter_sum((dot_back(d_gate, w_gate_s) + dot_back(d_up, w_up_s)).astype(bf16), ns)
    g_gate = scatter_grad(dot_rows(m_all, d_gate).astype(bf16))
    g_up = scatter_grad(dot_rows(m_all, d_up).astype(bf16))
    output = residual + scatter_sum(dot_plain(hidden, w_down_s).astype(bf16), ns)

    d_resid = cotangent[0].astype(f32) + scale_mlp * (
        d_normed - normed_mlp * jnp.mean(d_normed * normed_mlp, axis=-1, keepdims=True)
    )

    d_all = jnp.concatenate(gather_blocks(d_resid.astype(bf16), ns))
    d_gated = dot_back(d_all, w_out_s).astype(bf16)
    d_packed = attend_back(order, packed, d_gated, mixed, lse, cos_part, sin_part, start, ns)
    g_out = scatter_grad(columns_to_rows(dot_rows(gated, d_all).astype(bf16), ns))
    g_att = scatter_grad(dot_rows(n_all, d_packed).astype(bf16))
    d_normed2 = scatter_sum(dot_back(d_packed, w_att).astype(bf16), ns)
    scale_attn = inv_rms(inputs)
    normed_attn = inputs * scale_attn
    grad_tokens = d_resid + scale_attn * (
        d_normed2 - normed_attn * jnp.mean(d_normed2 * normed_attn, axis=-1, keepdims=True)
    )

    sum_down = join_rows(order, gather_blocks(g_down, ns), ns)
    sum_gate, sum_up, sum_gain_mlp = join_units(
        order, gather_blocks(g_gate, ns), gather_blocks(g_up, ns), w_gate, w_up, gain_mlp_f, ns, nf
    )
    sum_query, sum_key, sum_value, sum_attn_gate, sum_out, sum_gain_attn = join_attention(
        order, gather_blocks(g_att, ns), gather_blocks(g_out, ns), mats, gain_attn_f, ns
    )
    return (
        output.astype(bf16)[None],
        grad_tokens.astype(bf16)[None],
        sum_query,
        sum_key,
        sum_value,
        sum_attn_gate,
        sum_out,
        sum_gate,
        sum_up,
        sum_down,
        sum_gain_attn[:, 0],
        sum_gain_mlp[:, 0],
    )


def solution(mesh):
    row = P("fsdp", None)
    in_specs = (
        P("fsdp", "seq", None),
        row,
        row,
        P("fsdp", "seq", None),
    ) + (row,) * 8 + (P("fsdp"),) * 2
    out_specs = (P("fsdp", "seq", None),) * 2 + (row,) * 8 + (P("fsdp"),) * 2
    return jax.shard_map(
        functools.partial(shards, mesh.shape["seq"], mesh.shape["fsdp"]),
        mesh=mesh,
        in_specs=in_specs,
        out_specs=out_specs,
        check_vma=False,
    )
```
